32 devices in a mesh: row: 4 (over y, x), col: 8 (over z, core).
Axes of the slice: x: 2, y: 2, z: 4, core: 2. Of those that a mesh axis runs over, the one named last changes fastest.
Arguments:
- cov_inverse: float32 [14336, 14336], P('row', 'col'), may hold values from -0.020879785 to 4.0208798, as said below
- keys: bfloat16 [14336, 256], P(('row', 'col')), may hold values from -0.046875 to 0.046875
- residuals: bfloat16 [8192, 256], P('row', 'col'), may hold values from -24 to 24
- weights: bfloat16 [8192, 14336], P('row', 'col'), may hold values from -0.59765625 to 0.59765625
Outputs:
- edited: bfloat16 [8192, 14336], P('row', 'col')
The draws below stay inside these ranges and needn't reach their ends.
Inputs may be any that keep to these rules, and one draw needn't show every extreme that they name: `cov_inverse`: symmetric and positive definite, its diagonal dominating the remaining entries' action.
All inputs are finite; a program needn't handle non-finite values.
Results may differ from the reference program's by a relative error of at most 0.017.
Values may be sent and summed in bfloat16 or wider, within the bound.
No kernel may reach another device: no remote copies, remote signals or barrier semaphores. Data moves between devices by JAX's collectives and lax.ppermute only.
A program may use at most 128 MiB of HBM per device.

```python
import math
import jax
import jax.numpy as jnp
from jax import lax

D = 8192
F = 14336
FACTS = 256


def draw_cov_inverse(key, part):
    first = jax.random.fold_in(key, 11)
    second = jax.random.fold_in(key, 23)
    noise = jnp.clip(jax.random.normal(first, (F, F), jnp.float32), -6.0, 6.0)
    symmetric = (noise + noise.T) * (0.2 / math.sqrt(F))
    diagonal = jnp.exp(jax.random.uniform(second, (F,), jnp.float32, 0.0, math.log(4.0)))
    return symmetric + jnp.diag(diagonal)


def levels(own_key, shape, shards, smallest, largest):
    level, own = 1.0, jax.random.fold_in(own_key, 6)
    for dim, blocks in shards:
        steps = jnp.exp(jax.random.uniform(jax.random.fold_in(own, dim), (blocks,), jnp.float32, smallest / len(shards), largest / len(shards)))
        level = level * jnp.repeat(steps, shape[dim] // blocks).reshape([-1 if axis == dim else 1 for axis in range(len(shape))])
    return level


def bell_draw(rng, shape, scale, limit, split=(), kind=jnp.bfloat16):
    values = jax.random.normal(rng, shape, jnp.float32) * scale
    if len(split) > 0:
        values = levels(rng, shape, split, -0.22, 0.18) * values
    return jnp.clip(values, min=-limit, max=limit).astype(kind)


def setup_inputs(seed: int = 0) -> dict:
    key_of = jax.random.split(jax.random.key(seed), 5)
    return {
        "cov_inverse": draw_cov_inverse(jax.random.fold_in(key_of[4], 71), 0),
        "keys": bell_draw(key_of[1], (F, FACTS), F ** -0.5, 0.046875, ((0, 32),)),
        "residuals": bell_draw(key_of[2], (D, FACTS), 4.0, 24.0, ((0, 4), (1, 8))),
        "weights": bell_draw(key_of[3], (D, F), 0.1, 0.59765625, ((0, 4), (1, 8))),
    }


def reference(cov_inverse, keys, residuals, weights):
    wide_keys = keys.astype(jnp.float32)
    queries = jnp.dot(cov_inverse.astype(jnp.float32), wide_keys.astype(jnp.float32), precision=lax.Precision.HIGHEST, preferred_element_type=jnp.float32)
    gram = jnp.eye(FACTS, dtype=jnp.float32) + jnp.dot(wide_keys.T.astype(jnp.float32), queries.astype(jnp.float32), precision=lax.Precision.HIGHEST, preferred_element_type=jnp.float32)
    factor = jnp.linalg.cholesky(gram)
    solved = jax.scipy.linalg.cho_solve((factor, True), queries.T).T.astype(jnp.bfloat16)
    change = jnp.dot(residuals.astype(jnp.float32), solved.T.astype(jnp.float32), preferred_element_type=jnp.float32)
    return (weights.astype(jnp.float32) + change).astype(jnp.bfloat16)
```

```python
import jax
import jax.numpy as jnp
from jax import lax
from jax.experimental import pallas as pl
from jax.experimental.pallas import tpu as pltpu
from jax.sharding import PartitionSpec as P

BF, F32 = jnp.bfloat16, jnp.float32
NN = (((1,), (0,)), ((), ()))
TN = (((0,), (0,)), ((), ()))


def dot(a, b, dims=NN):
    return lax.dot_general(a, b, dims, preferred_element_type=F32)


def dot32(a, b):
    return lax.dot_general(
        a, b, NN, precision=lax.Precision.HIGHEST, preferred_element_type=F32
    )


def swap(x, axis, bits):
    size = lax.axis_size(axis)
    return lax.ppermute(x, axis, [(i, i ^ bits) for i in range(size)])


def query_kernel(rows_ref, key_a, key_b, cov_a, cov_b, *rest):
    out_ref, turned = rest[-2:]

    @pl.when(pl.program_id(0) == 0)
    def _():
        turned[0] = key_a[...].T
        turned[1] = key_b[...].T

    total = dot(turned[0], cov_a[...].astype(BF)) + dot(turned[1], cov_b[...].astype(BF))
    if len(rest) == 3:
        total = total + rest[0][...]
    out_ref[...] = total


def add_queries(total, key_a, key_b, rows, cov):
    block, facts = key_a.shape
    cols = cov.shape[1]
    tile = 256 if cols % 256 == 0 else cols
    key_spec = pl.BlockSpec((block, facts), lambda j, r: (0, 0))
    out_spec = pl.BlockSpec((facts, tile), lambda j, r: (0, j))
    in_specs = [
        key_spec,
        key_spec,
        pl.BlockSpec((block, tile), lambda j, r: (r[0], j)),
        pl.BlockSpec((block, tile), lambda j, r: (r[1], j)),
    ]
    args = [key_a, key_b, cov, cov]
    if total is not None:
        in_specs.append(out_spec)
        args.append(total)
    return pl.pallas_call(
        query_kernel,
        grid_spec=pltpu.PrefetchScalarGridSpec(
            num_scalar_prefetch=1,
            grid=(cols // tile,),
            in_specs=in_specs,
            out_specs=out_spec,
            scratch_shapes=[pltpu.VMEM((2, facts, block), BF)],
        ),
        out_shape=jax.ShapeDtypeStruct((facts, cols), F32),
        name="add_queries",
    )(rows, *args)


def gram_kernel(core_ref, total, keys, keep, send, low, high):
    facts, half = total.shape[0], keep.shape[0]
    wide = total[...]
    top = wide.astype(BF)
    rest = (wide - top.astype(F32)).astype(BF)
    column = keys[...]
    gram = dot(top, column) + dot(rest, column)
    core = core_ref[0]
    upper, lower = gram[:half], gram[half:]
    keep[...] = jnp.where(core == 0, upper, lower)
    send[...] = jnp.where(core == 0, lower, upper)
    low[...] = top[:half]
    high[...] = top[half:]


def gram_of(total, keys, core):
    facts, cols = total.shape
    half = facts // 2
    part = jax.ShapeDtypeStruct((half, facts), F32)
    query = jax.ShapeDtypeStruct((half, cols), BF)
    vmem = pl.BlockSpec(memory_space=pltpu.VMEM)
    return pl.pallas_call(
        gram_kernel,
        in_specs=[pl.BlockSpec(memory_space=pltpu.SMEM), vmem, vmem],
        out_specs=[vmem] * 4,
        out_shape=[part, part, query, query],
        name="gram_of",
    )(core, total, keys)


def eliminate(block):
    size = block.shape[0]
    row_at = lax.broadcasted_iota(jnp.int32, (size, size), 0)
    col_at = lax.broadcasted_iota(jnp.int32, (size, size), 1)
    lane = lax.broadcasted_iota(jnp.int32, (1, size), 1)
    for j in range(size):
        row, col, pivot = block[j : j + 1], block[:, j : j + 1], block[j : j + 1, j : j + 1]
        new = jnp.where(lane == j, 1.0, row) / pivot
        block = jnp.where(row_at == j, new, jnp.where(col_at == j, 0.0, block) - col * new)
    return block


def block_inverse(gram):
    half = gram.shape[0] // 2
    if gram.shape[0] <= 128:
        return eliminate(gram)
    first = block_inverse(gram[:half, :half])
    right = dot32(first, gram[:half, half:])
    left = dot32(gram[half:, :half], first)
    last = block_inverse(gram[half:, half:] - dot32(gram[half:, :half], right))
    upper = -dot32(right, last)
    lower = -dot32(last, left)
    corner = first - dot32(upper, left)
    return jnp.concatenate(
        [jnp.concatenate([corner, upper], 1), jnp.concatenate([lower, last], 1)], 0
    )


def inverse_kernel(core_ref, own, other, out, gram):
    half, facts = own.shape
    core = core_ref[0]
    row_at = lax.broadcasted_iota(jnp.int32, (facts, facts), 0)
    col_at = lax.broadcasted_iota(jnp.int32, (facts, facts), 1)
    eye = jnp.where(row_at == col_at, 1.0, 0.0)
    own_part, other_part = own[...], other[...]
    upper = jnp.where(core == 0, own_part, other_part)
    lower = jnp.where(core == 0, other_part, own_part)
    whole = jnp.concatenate([upper, lower], 0) + eye
    gram[...] = whole
    scale_row = 1.0 / jnp.sum(whole * eye, 0, keepdims=True)
    scale_col = 1.0 / jnp.sum(whole * eye, 1, keepdims=True)
    err = eye - whole * scale_row
    err_low = err.astype(BF)
    square = dot(err_low, err_low)
    first = eye + err
    guess = (first + dot(first.astype(BF), square.astype(BF))) * scale_col
    for _ in range(2):
        gap = eye - dot32(whole, guess)
        guess = guess + dot(guess.astype(BF), gap.astype(BF))
    out[...] = guess
    missed = jnp.sum(gap * gap)

    @pl.when(jnp.logical_not(missed < 1e-7))
    def _():
        out[...] = block_inverse(gram[...])


def inverse_of(own, other, core):
    half, facts = own.shape
    vmem = pl.BlockSpec(memory_space=pltpu.VMEM)
    return pl.pallas_call(
        inverse_kernel,
        in_specs=[pl.BlockSpec(memory_space=pltpu.SMEM), vmem, vmem],
        out_specs=vmem,
        out_shape=jax.ShapeDtypeStruct((facts, facts), F32),
        scratch_shapes=[pltpu.VMEM((facts, facts), F32)],
        name="inverse_of",
    )(core, own, other)


def edit_kernel(col_ref, own, other, inverse, low, high, weights, out, top, rest, queries):
    facts = inverse.shape[0]
    half = facts // 2

    @pl.when(pl.program_id(0) == 0)
    def _():
        col = col_ref[0]
        count = col_ref[1]
        width = facts // col_ref.shape[0]
        for slot in range(facts // width):
            first = 2 * slot if slot < facts // width // 2 else 2 * (slot - facts // width // 2) + 1
            source = jnp.bitwise_xor(col, first)
            piece = inverse[pl.ds(pl.multiple_of(source * width, width), width), :]
            big = piece.astype(BF)
            top[slot * width : (slot + 1) * width, :] = big
            rest[slot * width : (slot + 1) * width, :] = (piece - big.astype(F32)).astype(BF)
        queries[:half] = low[...]
        queries[half:] = high[...]

    mixed = dot(own[...], top[:half], TN) + dot(own[...], rest[:half], TN)
    mixed = mixed + dot(other[...], top[half:], TN) + dot(other[...], rest[half:], TN)
    change = dot(mixed.astype(BF), queries[...])
    out[...] = (weights[...].astype(F32) + change).astype(BF)


def edit(own, other, inverse, low, high, weights, col):
    rows, cols = weights.shape
    facts = inverse.shape[0]
    half = facts // 2
    tile = 256
    fixed = lambda shape: pl.BlockSpec(shape, lambda i, c: (0, 0))
    turned = pl.BlockSpec((half, tile), lambda i, c: (0, i))
    block = pl.BlockSpec((tile, cols), lambda i, c: (i, 0))
    return pl.pallas_call(
        edit_kernel,
        grid_spec=pltpu.PrefetchScalarGridSpec(
            num_scalar_prefetch=1,
            grid=(rows // tile,),
            in_specs=[
                turned,
                turned,
                fixed((facts, facts)),
                fixed((half, cols)),
                fixed((half, cols)),
                block,
            ],
            out_specs=block,
            scratch_shapes=[
                pltpu.VMEM((facts, facts), BF),
                pltpu.VMEM((facts, facts), BF),
                pltpu.VMEM((facts, cols), BF),
            ],
        ),
        out_shape=jax.ShapeDtypeStruct((rows, cols), BF),
        name="edit",
    )(col, own, other, inverse, low, high, weights)


def on_device(cov, keys, residuals, weights):
    n_row, n_col = lax.axis_size("row"), lax.axis_size("col")
    row, col = lax.axis_index("row"), lax.axis_index("col")
    core = (col % 2)[None].astype(jnp.int32)
    block, facts = keys.shape
    cols = cov.shape[1]
    row_bits = [1 << b for b in range(n_row.bit_length() - 1)]
    far_bits = [1 << b for b in range(1, n_col.bit_length() - 1)]

    pieces = {0: keys}
    for m in range(2, n_col, 2):
        pieces[m] = swap(keys, "col", m)
    moves = []
    for source in range(n_row * n_col):
        to_col, to_row = divmod(source, n_row)
        moves.append((source, to_row * n_col + to_col))
    mine = lax.ppermute(keys, ("row", "col"), moves)
    column = jnp.zeros((n_row * block, facts), BF)
    for m in range(n_row):
        piece = mine if m == 0 else swap(mine, "row", m)
        column = lax.dynamic_update_slice(column, piece, ((row ^ m) * block, 0))
    for m in range(0, n_col, 2):
        pieces[m + 1] = swap(pieces[m], "col", 1)

    total = None
    for m in range(0, n_col, 2):
        rows = jnp.stack([col ^ m, col ^ (m + 1)]).astype(jnp.int32)
        total = add_queries(total, pieces[m], pieces[m + 1], rows, cov)

    gram, send, low, high = gram_of(total, column, core)
    gram = gram + swap(send, "col", 1)
    for bits in row_bits:
        gram = gram + swap(gram, "row", bits)
    gram, low, high = lax.optimization_barrier((gram, low, high))
    for bits in far_bits:
        gram = gram + swap(gram, "col", bits)
    inverse = inverse_of(gram, swap(gram, "col", 1), core)

    def joined(a, b):
        return (a.astype(F32) + b.astype(F32)).astype(BF)

    for step in range(len(row_bits)):
        low_in = swap(low, "row", row_bits[step])
        high_in = swap(high, "row", row_bits[-1 - step])
        low, high = joined(low, low_in), joined(high, high_in)

    turned = residuals.T
    own = [turned] + [swap(turned, "col", m) for m in range(2, n_col, 2)]
    own = jnp.concatenate(own, 0)
    other = swap(own, "col", 1)
    index = jnp.full((n_col,), col, jnp.int32)
    return edit(own, other, inverse, low, high, weights, index)


def solution(mesh):
    in_specs = (P("row", "col"), P(("row", "col"), None), P("row", "col"), P("row", "col"))
    return jax.shard_map(
        on_device, mesh=mesh, in_specs=in_specs, out_specs=P("row", "col"), check_vma=False
    )
```
